32 devices in a mesh: band: 4 (over y, core), space: 8 (over z, x).
Axes of the slice: x: 2, y: 2, z: 4, core: 2. Of those that a mesh axis runs over, the one named last changes fastest.
Arguments:
- states: float32 [256, 48, 1024], P('band', 'space'), may hold values from -6 to 6
- patch_ids: int32 [48, 32], P('space'), may hold values from 0 to 63
- metric_table: float32 [64, 96], replicated, may hold values from 0.5 to 2
- potential: float32 [48, 1024], P('space'), may hold values from -3 to 0
Outputs:
- orthonormal: float32 [256, 48, 1024], P(None, 'space', 'band')
The draws below stay inside these ranges and needn't reach their ends.
All inputs are finite; a program needn't handle non-finite values.
Results may differ from the reference program's by a relative error of at most 0.00014.
Values sent between devices are 32-bit elements; how exact they have to be, the bound alone decides.
A program may use at most 64 MiB of HBM per device.

```python
import math
import jax
import jax.numpy as jnp
from jax import lax

STATES = 256
DEGREE = 3
PATCHES = 64
NY = 32
NZ = 32
NX = 48
NYZ = 1024
NCELLS = 49152
N_BAND = 4


def draw_potential(key, part):
    planes = (jnp.arange(NX, dtype=jnp.float32) + 0.5) / NX
    noise = jax.random.uniform(key, (NX, NY * NZ), jnp.float32, -1.0, 0.0)
    ramp = -2.0 * planes
    return noise + ramp[:, None]


def set_ends(values, stream_key, smallest, top_value):
    index_at = [jax.random.randint(jax.random.fold_in(stream_key, axis), (), 0, length) for axis, length in enumerate(values.shape)]
    main_axis = values.shape.index(max(values.shape))
    neighbour = index_at[:main_axis] + [(index_at[main_axis] + 1) % values.shape[main_axis]] + index_at[main_axis + 1:]
    return values.at[tuple(index_at)].set(smallest).at[tuple(neighbour)].set(top_value)


def level_of(rng, extent, split, smallest, high):
    def one(dim, blocks):
        steps = jax.random.uniform(jax.random.fold_in(jax.random.fold_in(rng, 6), dim), (blocks,), jnp.float32, smallest / len(split), high / len(split))
        return jnp.repeat(jnp.exp(steps), extent[dim] // blocks).reshape((-1,) + (1,) * (len(extent) - dim - 1))

    level = one(*split[0])
    for cut in split[1:]:
        level = level * one(*cut)
    return level


def scatter_about(key, dims, scale, bound, split=(), held_as=jnp.bfloat16):
    values = scale * jax.random.normal(key, dims, jnp.float32)
    if split:
        values = values * level_of(key, dims, split, -0.22, 0.18)
    return jnp.clip(values, -bound, bound).astype(held_as)


def setup_inputs(seed: int = 0) -> dict:
    keys = jax.random.split(jax.random.key(seed), 5)
    states = scatter_about(keys[0], (STATES, NX, NYZ), 1.0, 6.0, ((0, 4), (1, 8)), jnp.float32)
    patch_ids = set_ends(jax.random.randint(keys[1], (NX, NY), 0, PATCHES), jax.random.fold_in(keys[1], 1), 0, PATCHES - 1).astype(jnp.int32)
    metric_table = jnp.clip(jnp.exp(jax.random.uniform(keys[2], (PATCHES, 3 * NZ), jnp.float32, math.log(0.5), math.log(2.0))), 0.5, 2.0)
    potential = draw_potential(jax.random.fold_in(keys[4], 71), 0)
    return {"states": states, "patch_ids": patch_ids, "metric_table": metric_table, "potential": potential}


CENTRE = 8.5
HALF_WIDTH = 7.5
OFFSETS = (-2, -1, 0, 1, 2)
WEIGHTS = (-1.0 / 12.0, 4.0 / 3.0, -2.5, 4.0 / 3.0, -1.0 / 12.0)

def second_difference(padded, axis, length):
    total = WEIGHTS[0] * lax.slice_in_dim(padded, 2 + OFFSETS[0], 2 + OFFSETS[0] + length, axis=axis)
    for offset, weight in zip(OFFSETS[1:], WEIGHTS[1:]):
        total = total + weight * lax.slice_in_dim(padded, 2 + offset, 2 + offset + length, axis=axis)
    return total

def hamiltonian(block, pot_grid, metric):
    x_pad = jnp.pad(block, ((0, 0), (2, 2), (0, 0), (0, 0)))
    y_pad = jnp.pad(block, ((0, 0), (0, 0), (2, 2), (0, 0)))
    z_pad = jnp.pad(block, ((0, 0), (0, 0), (0, 0), (2, 2)))
    x_term = second_difference(x_pad, 1, block.shape[1])
    y_term = second_difference(y_pad, 2, block.shape[2])
    z_term = second_difference(z_pad, 3, block.shape[3])
    kinetic = metric[0] * x_term + metric[1] * y_term + metric[2] * z_term
    return pot_grid * block - 0.5 * kinetic

def chebyshev(block, pot_grid, metric):
    applied = hamiltonian(block, pot_grid, metric)
    earlier = block
    current = (applied - CENTRE * block) / HALF_WIDTH
    for degree_step in range(DEGREE - 1):
        applied = hamiltonian(current, pot_grid, metric)
        following = 2.0 * (applied - CENTRE * current) / HALF_WIDTH - earlier
        earlier = current
        current = following
    return current

def reference(states, patch_ids, metric_table, potential):
    looked = metric_table[patch_ids]
    metric = looked.reshape(NX, NY, 3, NZ).transpose(2, 0, 1, 3)
    pot_grid = potential.reshape(NX, NY, NZ)
    group = STATES // N_BAND
    blocks = states.reshape(STATES // group, group, NX, NY, NZ)
    filtered = lax.map(lambda block: chebyshev(block, pot_grid, metric), blocks)
    flat = filtered.reshape(STATES, NX * NY * NZ)
    gram = jnp.dot(flat.astype(jnp.float32), flat.T.astype(jnp.float32), precision=lax.Precision.HIGHEST, preferred_element_type=jnp.float32) / NCELLS
    factor = jnp.linalg.cholesky(gram)
    result = lax.linalg.triangular_solve(factor, flat, left_side=True, lower=True)
    return result.reshape(STATES, NX, NY * NZ)
```

```python
import functools

import jax
import jax.numpy as jnp
from jax import lax
from jax.experimental import pallas as pl
from jax.experimental.pallas import tpu as pltpu
from jax.sharding import PartitionSpec as P

DEGREE = 3
NY = 32
NZ = 32


CENTRE = 8.5
HALF_WIDTH = 7.5
OFFSETS = (-2, -1, 0, 1, 2)
WEIGHTS = (-1.0 / 12.0, 4.0 / 3.0, -2.5, 4.0 / 3.0, -1.0 / 12.0)


def with_halo(cells, sides, width):
    for axis, dim in sides:
        count = lax.axis_size(axis)
        ends = count - 1
        head = lax.slice_in_dim(cells, 0, width, axis=dim)
        tail = lax.slice_in_dim(cells, cells.shape[dim] - width, cells.shape[dim], axis=dim)
        cells = jnp.concatenate(
            [
                lax.ppermute(tail, axis, [(i, (i + 1) % count) for i in range(ends)]),
                cells,
                lax.ppermute(head, axis, [((i + 1) % count, i) for i in range(ends)]),
            ],
            axis=dim,
        )
    return cells


MESH = pl.DeviceIdType.MESH
HIGHEST = lax.Precision.HIGHEST
BLOCK = 64
TILE = 8


def matmul(left, right, dims):
    return lax.dot_general(
        left, right, (dims, ((), ())), precision=HIGHEST, preferred_element_type=jnp.float32
    )


def factor_block(diagonal):
    size = diagonal.shape[0]
    rows = lax.broadcasted_iota(jnp.int32, (size, size), 0)
    columns = lax.broadcasted_iota(jnp.int32, (size, size), 1)
    unit = jnp.where(rows == columns, 1.0, 0.0).astype(jnp.float32)
    work = jnp.concatenate([diagonal, unit], axis=1)
    width = work.shape[1]
    in_tile = lax.broadcasted_iota(jnp.int32, (TILE, width), 0)
    done = []
    for start in range(0, size, TILE):
        count = size - start
        row_in = lax.broadcasted_iota(jnp.int32, (count, width), 0)
        panel = [
            jnp.broadcast_to(work[:, start + k : start + k + 1], (count, width))
            for k in range(TILE)
        ]
        scale = jnp.zeros((TILE, width), jnp.float32)
        for k in range(TILE):
            pivot = panel[k][k : k + 1, :]
            inverse = 1.0 / pivot
            scale = jnp.where(in_tile == k, 1.0 / jnp.sqrt(pivot), scale)
            weight = jnp.where(row_in > k, panel[k] * inverse, 0.0)
            for later in range(k + 1, TILE):
                panel[later] = panel[later] - weight * panel[later][k : k + 1, :]
            work = work - weight * work[k : k + 1, :]
        done.append(work[:TILE] * scale)
        work = work[TILE:]
    return jnp.concatenate(done, axis=0)[:, size:]


def inverse_factor(work_ref, size):
    rows = lax.broadcasted_iota(jnp.int32, (size, size), 0)
    columns = lax.broadcasted_iota(jnp.int32, (size, size), 1)
    work_ref[:, size:] = jnp.where(rows == columns, 1.0, 0.0).astype(jnp.float32)
    for first in range(0, size, BLOCK):
        last = first + BLOCK
        low = first // 128 * 128
        high = size + -(-last // 128) * 128
        small = factor_block(work_ref[first:last, first:last])
        solved = matmul(small, work_ref[first:last, low:high], ((1,), (0,)))
        work_ref[first:last, low:high] = solved
        if last < size:
            aligned = last // 128 * 128
            update = matmul(solved[:, aligned - low : size - low], solved, ((0,), (0,)))
            work_ref[last:, low:high] -= update[last - aligned :]


def factor_kernel(axes, cell_total, gram_ref, out_ref, parts, mine, work, send_sems, recv_sems):
    size = gram_ref.shape[0]
    if axes:
        (outer, outer_size), (inner, inner_size) = axes
        count = outer_size * inner_size
        share = size // count
        me = lax.axis_index(outer) * inner_size + lax.axis_index(inner)

        def peer(offset):
            index = lax.rem(me + offset, count)
            return index, {outer: index // inner_size, inner: lax.rem(index, inner_size)}

        barrier = pltpu.get_barrier_semaphore()
        for offset in range(1, count):
            pl.semaphore_signal(barrier, inc=1, device_id=peer(offset)[1], device_id_type=MESH)
        pl.semaphore_wait(barrier, count - 1)
        for offset in range(1, count):
            index, target = peer(offset)
            pltpu.make_async_remote_copy(
                src_ref=gram_ref.at[pl.ds(pl.multiple_of(index * share, share), share)],
                dst_ref=parts.at[offset - 1],
                send_sem=send_sems.at[0],
                recv_sem=recv_sems.at[0],
                device_id=target,
                device_id_type=MESH,
            ).start()
        own = pl.ds(pl.multiple_of(me * share, share), share)
        pltpu.make_async_copy(parts, parts, recv_sems.at[0]).wait()
        mine[...] = (jnp.sum(parts[...], axis=0) + gram_ref[own]) / cell_total
        for offset in range(1, count):
            index, target = peer(offset)
            pltpu.make_async_remote_copy(
                src_ref=mine,
                dst_ref=work.at[own, 0:size],
                send_sem=send_sems.at[1],
                recv_sem=recv_sems.at[1],
                device_id=target,
                device_id_type=MESH,
            ).start()
        pltpu.make_async_copy(parts, parts, send_sems.at[0]).wait()
        others = work.at[0 : size - share, 0:size]
        pltpu.make_async_copy(others, others, recv_sems.at[1]).wait()
        work[own, 0:size] = mine[...]
        pltpu.make_async_copy(parts, parts, send_sems.at[1]).wait()
    else:
        work[:, 0:size] = gram_ref[...] / cell_total
    inverse_factor(work, size)
    out_ref[...] = work[:, size:]


def inverse_of_gram(gram, cell_total):
    size = gram.shape[0]
    axes = tuple((name, lax.axis_size(name)) for name in ("band", "space"))
    count = axes[0][1] * axes[1][1]
    direct = size % (count * TILE) == 0
    if not direct:
        gram = lax.psum(gram, ("band", "space"))
    share = size // count if direct else TILE
    peers = count - 1 if direct else 1
    return pl.pallas_call(
        functools.partial(factor_kernel, axes if direct else (), float(cell_total)),
        out_shape=jax.ShapeDtypeStruct((size, size), jnp.float32),
        in_specs=[pl.BlockSpec(memory_space=pltpu.VMEM)],
        out_specs=pl.BlockSpec(memory_space=pltpu.VMEM),
        scratch_shapes=[
            pltpu.VMEM((peers, share, size), jnp.float32),
            pltpu.VMEM((share, size), jnp.float32),
            pltpu.VMEM((size, 2 * size), jnp.float32),
            pltpu.SemaphoreType.DMA((2,)),
            pltpu.SemaphoreType.DMA((2,)),
        ],
        compiler_params=pltpu.CompilerParams(
            collective_id=1 if direct else None, has_side_effects=direct
        ),
        name="gram_factor",
    )(gram)


def apply_ham(extended, potential, metric, z_weights):
    planes = extended.shape[1] - 4
    plane_cells = extended.shape[2]
    block = extended[:, 2 : 2 + planes, :]
    row_pad = 2 * NZ
    padded = jnp.pad(block, ((0, 0), (0, 0), (row_pad, row_pad)))
    x_term = WEIGHTS[0] * extended[:, 2 + OFFSETS[0] : 2 + OFFSETS[0] + planes, :]
    y_term = (
        WEIGHTS[0]
        * padded[:, :, row_pad + OFFSETS[0] * NZ : row_pad + OFFSETS[0] * NZ + plane_cells]
    )
    z_term = z_weights[0] * padded[:, :, row_pad + OFFSETS[0] : row_pad + OFFSETS[0] + plane_cells]
    for position in range(1, 5):
        offset = OFFSETS[position]
        weight = WEIGHTS[position]
        x_term = x_term + weight * extended[:, 2 + offset : 2 + offset + planes, :]
        y_term = (
            y_term
            + weight * padded[:, :, row_pad + offset * NZ : row_pad + offset * NZ + plane_cells]
        )
        z_term = (
            z_term
            + z_weights[position] * padded[:, :, row_pad + offset : row_pad + offset + plane_cells]
        )
    kinetic = metric[0] * x_term + metric[1] * y_term + metric[2] * z_term
    return potential * block - 0.5 * kinetic


def on_device(states, patch_ids, metric_table, potential):
    planes = states.shape[1]
    plane_cells = states.shape[2]
    one_hot = (patch_ids[:, :, None] == jnp.arange(metric_table.shape[0], dtype=jnp.int32)).astype(
        jnp.float32
    )
    looked = jnp.einsum("xyp,pm->xym", one_hot, metric_table, precision=lax.Precision.HIGHEST)
    metric = looked.reshape(planes, NY, 3, NZ).transpose(2, 0, 1, 3).reshape(3, planes, plane_cells)
    z_index = jnp.arange(plane_cells, dtype=jnp.int32) % NZ
    z_weights = [
        WEIGHTS[position]
        * ((z_index + OFFSETS[position] >= 0) & (z_index + OFFSETS[position] < NZ)).astype(
            jnp.float32
        )
        for position in range(5)
    ]

    def step_ham(block):
        extended = with_halo(block, (("space", 1),), 2)
        return apply_ham(extended, potential, metric, z_weights)

    applied = step_ham(states)
    earlier = states
    current = (applied - CENTRE * states) / HALF_WIDTH
    for degree_step in range(DEGREE - 1):
        applied = step_ham(current)
        following = 2.0 * (applied - CENTRE * current) / HALF_WIDTH - earlier
        earlier = current
        current = following
    regrouped = lax.all_to_all(current, "band", split_axis=2, concat_axis=0, tiled=True)
    all_states = regrouped.shape[0]
    flat = regrouped.reshape(all_states, -1)
    cell_total = planes * plane_cells * lax.axis_size("space")
    local_gram = jnp.dot(
        flat, flat.T, precision=lax.Precision.HIGHEST, preferred_element_type=jnp.float32
    )
    inverse = inverse_of_gram(local_gram, cell_total)
    result = jnp.dot(
        inverse, flat, precision=lax.Precision.HIGHEST, preferred_element_type=jnp.float32
    )
    return result.reshape(all_states, planes, regrouped.shape[2])


def solution(mesh):
    return jax.shard_map(
        on_device,
        mesh=mesh,
        in_specs=(P("band", "space", None), P("space", None), P(), P("space", None)),
        out_specs=P(None, "space", "band"),
        check_vma=False,
    )
```

```python
import functools

import jax
import jax.numpy as jnp
from jax import lax
from jax.experimental import pallas as pl
from jax.experimental.pallas import tpu as pltpu
from jax.sharding import PartitionSpec as P

DEGREE = 3
NY = 32
NZ = 32


CENTRE = 8.5
HALF_WIDTH = 7.5
OFFSETS = (-2, -1, 0, 1, 2)
WEIGHTS = (-1.0 / 12.0, 4.0 / 3.0, -2.5, 4.0 / 3.0, -1.0 / 12.0)


MESH = pl.DeviceIdType.MESH
HIGHEST = lax.Precision.HIGHEST
BLOCK = 64
TILE = 8


def matmul(left, right, dims):
    return lax.dot_general(
        left, right, (dims, ((), ())), precision=HIGHEST, preferred_element_type=jnp.float32
    )


def factor_block(diagonal):
    size = diagonal.shape[0]
    rows = lax.broadcasted_iota(jnp.int32, (size, size), 0)
    columns = lax.broadcasted_iota(jnp.int32, (size, size), 1)
    unit = jnp.where(rows == columns, 1.0, 0.0).astype(jnp.float32)
    work = jnp.concatenate([diagonal, unit], axis=1)
    width = work.shape[1]
    in_tile = lax.broadcasted_iota(jnp.int32, (TILE, width), 0)
    done = []
    for start in range(0, size, TILE):
        count = size - start
        row_in = lax.broadcasted_iota(jnp.int32, (count, width), 0)
        panel = [
            jnp.broadcast_to(work[:, start + k : start + k + 1], (count, width))
            for k in range(TILE)
        ]
        scale = jnp.zeros((TILE, width), jnp.float32)
        for k in range(TILE):
            pivot = panel[k][k : k + 1, :]
            inverse = 1.0 / pivot
            scale = jnp.where(in_tile == k, 1.0 / jnp.sqrt(pivot), scale)
            weight = jnp.where(row_in > k, panel[k] * inverse, 0.0)
            for later in range(k + 1, TILE):
                panel[later] = panel[later] - weight * panel[later][k : k + 1, :]
            work = work - weight * work[k : k + 1, :]
        done.append(work[:TILE] * scale)
        work = work[TILE:]
    return jnp.concatenate(done, axis=0)[:, size:]


def inverse_factor(work_ref, size):
    rows = lax.broadcasted_iota(jnp.int32, (size, size), 0)
    columns = lax.broadcasted_iota(jnp.int32, (size, size), 1)
    work_ref[:, size:] = jnp.where(rows == columns, 1.0, 0.0).astype(jnp.float32)
    for first in range(0, size, BLOCK):
        last = first + BLOCK
        low = first // 128 * 128
        high = size + -(-last // 128) * 128
        small = factor_block(work_ref[first:last, first:last])
        solved = matmul(small, work_ref[first:last, low:high], ((1,), (0,)))
        work_ref[first:last, low:high] = solved
        if last < size:
            aligned = last // 128 * 128
            update = matmul(solved[:, aligned - low : size - low], solved, ((0,), (0,)))
            work_ref[last:, low:high] -= update[last - aligned :]


def factor_kernel(axes, cell_total, gram_ref, out_ref, parts, mine, work, send_sems, recv_sems):
    size = gram_ref.shape[0]
    if axes:
        (outer, outer_size), (inner, inner_size) = axes
        count = outer_size * inner_size
        share = size // count
        me = lax.axis_index(outer) * inner_size + lax.axis_index(inner)

        def peer(offset):
            index = lax.rem(me + offset, count)
            return index, {outer: index // inner_size, inner: lax.rem(index, inner_size)}

        barrier = pltpu.get_barrier_semaphore()
        for offset in range(1, count):
            pl.semaphore_signal(barrier, inc=1, device_id=peer(offset)[1], device_id_type=MESH)
        pl.semaphore_wait(barrier, count - 1)
        for offset in range(1, count):
            index, target = peer(offset)
            pltpu.make_async_remote_copy(
                src_ref=gram_ref.at[pl.ds(pl.multiple_of(index * share, share), share)],
                dst_ref=parts.at[offset - 1],
                send_sem=send_sems.at[0],
                recv_sem=recv_sems.at[0],
                device_id=target,
                device_id_type=MESH,
            ).start()
        own = pl.ds(pl.multiple_of(me * share, share), share)
        pltpu.make_async_copy(parts, parts, recv_sems.at[0]).wait()
        mine[...] = (jnp.sum(parts[...], axis=0) + gram_ref[own]) / cell_total
        for offset in range(1, count):
            index, target = peer(offset)
            pltpu.make_async_remote_copy(
                src_ref=mine,
                dst_ref=work.at[own, 0:size],
                send_sem=send_sems.at[1],
                recv_sem=recv_sems.at[1],
                device_id=target,
                device_id_type=MESH,
            ).start()
        pltpu.make_async_copy(parts, parts, send_sems.at[0]).wait()
        others = work.at[0 : size - share, 0:size]
        pltpu.make_async_copy(others, others, recv_sems.at[1]).wait()
        work[own, 0:size] = mine[...]
        pltpu.make_async_copy(parts, parts, send_sems.at[1]).wait()
    else:
        work[:, 0:size] = gram_ref[...] / cell_total
    inverse_factor(work, size)
    out_ref[...] = work[:, size:]


def inverse_of_gram(gram, cell_total):
    size = gram.shape[0]
    axes = tuple((name, lax.axis_size(name)) for name in ("band", "space"))
    count = axes[0][1] * axes[1][1]
    direct = size % (count * TILE) == 0
    if not direct:
        gram = lax.psum(gram, ("band", "space"))
    share = size // count if direct else TILE
    peers = count - 1 if direct else 1
    return pl.pallas_call(
        functools.partial(factor_kernel, axes if direct else (), float(cell_total)),
        out_shape=jax.ShapeDtypeStruct((size, size), jnp.float32),
        in_specs=[pl.BlockSpec(memory_space=pltpu.VMEM)],
        out_specs=pl.BlockSpec(memory_space=pltpu.VMEM),
        scratch_shapes=[
            pltpu.VMEM((peers, share, size), jnp.float32),
            pltpu.VMEM((share, size), jnp.float32),
            pltpu.VMEM((size, 2 * size), jnp.float32),
            pltpu.SemaphoreType.DMA((2,)),
            pltpu.SemaphoreType.DMA((2,)),
        ],
        compiler_params=pltpu.CompilerParams(
            collective_id=1 if direct else None, has_side_effects=direct
        ),
        name="gram_factor",
    )(gram)


FIRST = 4.0 / 3.0
SECOND = -1.0 / 12.0
REACH = 2


def order_of(chunks, steps):
    pairs = [(chunk, step) for chunk in range(chunks) for step in range(steps)]
    return sorted(pairs, key=lambda pair: (pair[0] + pair[1], -pair[1]))


def filter_kernel(
    bands, spaces, states, base, shift_weights, out, grids, last, cells, base_sems,
    in_send, in_recv, own_sems, halo_send, halo_recv, out_send, out_recv,
):
    planes, held, plane_cells = states.shape
    half = held // 2
    chunks = half // TILE
    both = 2 * planes
    share = plane_cells // bands
    band = lax.axis_index("band")
    space = lax.axis_index("space")
    side = lax.rem(space, 2)
    partner = space + 1 - 2 * side
    ends = {0: space >= 2, 1: space < spaces - 2}
    towards = {0: space - 2, 1: space + 2}

    def to(target_band, target_space):
        return {"band": target_band, "space": target_space}

    barrier = pltpu.get_barrier_semaphore()
    for turn in range(bands):
        target = lax.rem(band + turn, bands)
        if turn:
            pl.semaphore_signal(
                barrier, inc=1, device_id=to(target, space), device_id_type=MESH
            )
        pl.semaphore_signal(barrier, inc=1, device_id=to(target, partner), device_id_type=MESH)
    for end in (0, 1):

        @pl.when(ends[end])
        def _():
            pl.semaphore_signal(
                barrier, inc=1, device_id=to(band, towards[end]), device_id_type=MESH
            )

    below = jnp.minimum(space // 2, 1)
    above = jnp.minimum((spaces - 1 - space) // 2, 1)
    pl.semaphore_wait(barrier, 2 * bands - 1 + below + above)

    own_planes = pl.ds(REACH + side * planes, planes)
    base_out = pltpu.make_async_remote_copy(
        src_ref=base,
        dst_ref=cells.at[side],
        send_sem=base_sems.at[0],
        recv_sem=base_sems.at[1],
        device_id=to(band, partner),
        device_id_type=MESH,
    )
    base_own = pltpu.make_async_copy(base, cells.at[side], base_sems.at[2])
    enter, keep = [], []
    for chunk in range(chunks):
        given = pl.ds(pl.multiple_of((1 - side) * half + chunk * TILE, TILE), TILE)
        kept = pl.ds(pl.multiple_of(side * half + chunk * TILE, TILE), TILE)
        enter.append(
            pltpu.make_async_remote_copy(
                src_ref=states.at[:, given],
                dst_ref=grids.at[0, chunk, own_planes],
                send_sem=in_send.at[chunk],
                recv_sem=in_recv.at[chunk],
                device_id=to(band, partner),
                device_id_type=MESH,
            )
        )
        keep.append(
            pltpu.make_async_copy(
                states.at[:, kept], grids.at[0, chunk, own_planes], own_sems.at[chunk]
            )
        )
    enter[0].start()
    base_out.start()
    base_own.start()
    keep[0].start()
    for chunk in range(1, chunks):
        enter[chunk].start()
        keep[chunk].start()

    for end in (0, 1):

        @pl.when(jnp.logical_not(ends[end]))
        def _():
            edge = end * (both + REACH)
            for step in range(DEGREE):
                for chunk in range(chunks):
                    grids[step, chunk, edge : edge + REACH] = jnp.zeros(
                        (REACH, TILE, plane_cells), jnp.float32
                    )

    def halo(step, chunk, end):
        source = REACH if end == 0 else both
        landing = both + REACH if end == 0 else 0
        return pltpu.make_async_remote_copy(
            src_ref=grids.at[step, chunk, source : source + REACH],
            dst_ref=grids.at[step, chunk, landing : landing + REACH],
            send_sem=halo_send.at[step, chunk, end],
            recv_sem=halo_recv.at[step, chunk, end],
            device_id=to(band, towards[end]),
            device_id_type=MESH,
        )

    def landed(step, chunk, end):
        landing = 0 if end == 0 else both + REACH
        return pltpu.make_async_copy(
            grids.at[step, chunk, landing : landing + REACH],
            grids.at[step, chunk, landing : landing + REACH],
            halo_recv.at[step, chunk, 1 - end],
        )

    def send_halos(step, chunk):
        for end in (0, 1):

            @pl.when(ends[end])
            def _():
                halo(step, chunk, end).start()

    def apply(step, chunk):
        def plane(index, carry):
            here = REACH + index
            slab = index // planes
            row = pl.ds(index - slab * planes, 1)
            value = grids[step, chunk, here]
            near = grids[step, chunk, here - 1] + grids[step, chunk, here + 1]
            far = grids[step, chunk, here - 2] + grids[step, chunk, here + 2]
            total = cells[slab, 0, row] * value
            total = total + cells[slab, 1, row] * (FIRST * near + SECOND * far)
            for kind, stride in ((0, NZ), (1, 1)):
                part = None
                for position, offset in enumerate((-2, -1, 1, 2)):
                    amount = (-offset * stride) % plane_cells
                    moved = pltpu.roll(value, amount, axis=1)
                    number = kind * 4 + position
                    term = shift_weights[number : number + 1] * moved
                    part = term if part is None else part + term
                total = total + cells[slab, 2 + kind, row] * part
            if step > 0:
                total = 2.0 * total - grids[step - 1, chunk, here]
            if step < DEGREE - 1:
                grids[step + 1, chunk, here] = total
            else:
                last[chunk, index] = total
            return carry

        lax.fori_loop(0, both, plane, 0)

    def leave(chunk):
        rows = pl.ds(pl.multiple_of(band * held + side * half + chunk * TILE, TILE), TILE)
        for turn in range(bands):
            target = lax.rem(band + turn, bands)
            columns = pl.ds(pl.multiple_of(target * share, share), share)
            for other in (1, 0):
                slab = side if other == 0 else 1 - side
                source = last.at[chunk, pl.ds(slab * planes, planes), :, columns]
                landing = out.at[:, rows, :]
                if turn == 0 and other == 0:
                    pltpu.make_async_copy(source, landing, out_recv.at[0]).start()
                else:
                    pltpu.make_async_remote_copy(
                        src_ref=source,
                        dst_ref=landing,
                        send_sem=out_send.at[0],
                        recv_sem=out_recv.at[0],
                        device_id=to(target, space if other == 0 else partner),
                        device_id_type=MESH,
                    ).start()

    for chunk, step in order_of(chunks, DEGREE):
        if step == 0:
            if chunk == 0:
                base_own.wait()
                base_out.wait_recv()
            keep[chunk].wait()
            enter[chunk].wait_recv()
            send_halos(0, chunk)
        for end in (0, 1):

            @pl.when(ends[end])
            def _():
                landed(step, chunk, end).wait()

        apply(step, chunk)
        if step < DEGREE - 1:
            send_halos(step + 1, chunk)
        else:
            leave(chunk)

    base_out.wait_send()
    for chunk in range(chunks):
        enter[chunk].wait_send()
        for step in range(DEGREE):
            for end in (0, 1):

                @pl.when(ends[end])
                def _():
                    halo(step, chunk, end).wait_send()

    pltpu.make_async_copy(out, out, out_recv.at[0]).wait()
    sent = out.at[:, 0 : out.shape[1] - out.shape[1] // (2 * bands), :]
    pltpu.make_async_copy(sent, sent, out_send.at[0]).wait()


def filtered_and_regrouped(states, base, shift_weights):
    planes, held, plane_cells = states.shape
    bands = lax.axis_size("band")
    spaces = lax.axis_size("space")
    chunks = held // 2 // TILE
    both = 2 * planes
    dma = pltpu.SemaphoreType.DMA
    return pl.pallas_call(
        functools.partial(filter_kernel, bands, spaces),
        out_shape=jax.ShapeDtypeStruct((planes, held * bands, plane_cells // bands), jnp.float32),
        in_specs=[
            pl.BlockSpec(memory_space=pl.ANY),
            pl.BlockSpec(memory_space=pltpu.VMEM),
            pl.BlockSpec(memory_space=pltpu.VMEM),
        ],
        out_specs=pl.BlockSpec(memory_space=pl.ANY),
        scratch_shapes=[
            pltpu.VMEM((DEGREE, chunks, both + 2 * REACH, TILE, plane_cells), jnp.float32),
            pltpu.VMEM((chunks, both, TILE, plane_cells), jnp.float32),
            pltpu.VMEM((2,) + base.shape, jnp.float32),
            dma((3,)),
            dma((chunks,)),
            dma((chunks,)),
            dma((chunks,)),
            dma((DEGREE, chunks, 2)),
            dma((DEGREE, chunks, 2)),
            dma((1,)),
            dma((1,)),
        ],
        compiler_params=pltpu.CompilerParams(
            collective_id=0, has_side_effects=True, vmem_limit_bytes=40 * 2**20
        ),
        name="filter_regroup",
    )(states, base, shift_weights)


def coefficients(patch_ids, metric_table, potential):
    planes, plane_cells = potential.shape
    one_hot = (patch_ids[:, :, None] == jnp.arange(metric_table.shape[0], dtype=jnp.int32)).astype(
        jnp.float32
    )
    looked = jnp.einsum("xyp,pm->xym", one_hot, metric_table, precision=HIGHEST)
    metric = looked.reshape(planes, NY, 3, NZ).transpose(2, 0, 1, 3).reshape(3, planes, plane_cells)
    kinetic = metric * (-0.5 / HALF_WIDTH)
    centre = (potential - CENTRE) / HALF_WIDTH + WEIGHTS[2] * (
        kinetic[0] + kinetic[1] + kinetic[2]
    )
    base = jnp.concatenate([centre[None], kinetic], axis=0)
    return jnp.pad(base, ((0, 0), (0, -planes % TILE), (0, 0)))


def on_device(states, patch_ids, metric_table, potential):
    planes, plane_cells = potential.shape
    index = jnp.arange(plane_cells, dtype=jnp.int32)
    rows = []
    for place in (index // NZ, index % NZ):
        length = NY if not rows else NZ
        for offset, weight in ((-2, SECOND), (-1, FIRST), (1, FIRST), (2, SECOND)):
            inside = (place + offset >= 0) & (place + offset < length)
            rows.append(jnp.where(inside, weight, 0.0).astype(jnp.float32))
    shift_weights = jnp.stack(rows)
    base = coefficients(patch_ids, metric_table, potential)
    filtered = filtered_and_regrouped(states.transpose(1, 0, 2), base, shift_weights)
    cell_total = planes * plane_cells * lax.axis_size("space")
    local_gram = lax.dot_general(
        filtered[0], filtered[0], (((1,), (1,)), ((), ())), precision=HIGHEST,
        preferred_element_type=jnp.float32,
    )
    for plane in range(1, planes):
        local_gram = local_gram + lax.dot_general(
            filtered[plane], filtered[plane], (((1,), (1,)), ((), ())), precision=HIGHEST,
            preferred_element_type=jnp.float32,
        )
    inverse = inverse_of_gram(local_gram, cell_total)
    result = jnp.einsum(
        "ts,psc->ptc", inverse, filtered, precision=HIGHEST, preferred_element_type=jnp.float32
    )
    return result.transpose(1, 0, 2)


def solution(mesh):
    return jax.shard_map(
        on_device,
        mesh=mesh,
        in_specs=(P("band", "space", None), P("space", None), P(), P("space", None)),
        out_specs=P(None, "space", "band"),
        check_vma=False,
    )
```

```python
import functools

import jax
import jax.numpy as jnp
from jax import lax
from jax.experimental import pallas as pl
from jax.experimental.pallas import tpu as pltpu
from jax.sharding import PartitionSpec as P

DEGREE = 3
NY = 32
NZ = 32


CENTRE = 8.5
HALF_WIDTH = 7.5
OFFSETS = (-2, -1, 0, 1, 2)
WEIGHTS = (-1.0 / 12.0, 4.0 / 3.0, -2.5, 4.0 / 3.0, -1.0 / 12.0)


MESH = pl.DeviceIdType.MESH
HIGHEST = lax.Precision.HIGHEST
BLOCK = 64
TILE = 8


def matmul(left, right, dims):
    return lax.dot_general(
        left, right, (dims, ((), ())), precision=HIGHEST, preferred_element_type=jnp.float32
    )


def factor_block(diagonal):
    size = diagonal.shape[0]
    rows = lax.broadcasted_iota(jnp.int32, (size, size), 0)
    columns = lax.broadcasted_iota(jnp.int32, (size, size), 1)
    unit = jnp.where(rows == columns, 1.0, 0.0).astype(jnp.float32)
    work = jnp.concatenate([diagonal, unit], axis=1)
    width = work.shape[1]
    in_tile = lax.broadcasted_iota(jnp.int32, (TILE, width), 0)
    done = []
    for start in range(0, size, TILE):
        count = size - start
        row_in = lax.broadcasted_iota(jnp.int32, (count, width), 0)
        panel = [
            jnp.broadcast_to(work[:, start + k : start + k + 1], (count, width))
            for k in range(TILE)
        ]
        scale = jnp.zeros((TILE, width), jnp.float32)
        for k in range(TILE):
            pivot = panel[k][k : k + 1, :]
            inverse = 1.0 / pivot
            scale = jnp.where(in_tile == k, 1.0 / jnp.sqrt(pivot), scale)
            weight = jnp.where(row_in > k, panel[k] * inverse, 0.0)
            for later in range(k + 1, TILE):
                panel[later] = panel[later] - weight * panel[later][k : k + 1, :]
            work = work - weight * work[k : k + 1, :]
        done.append(work[:TILE] * scale)
        work = work[TILE:]
    return jnp.concatenate(done, axis=0)[:, size:]


def inverse_factor(work_ref, size):
    rows = lax.broadcasted_iota(jnp.int32, (size, size), 0)
    columns = lax.broadcasted_iota(jnp.int32, (size, size), 1)
    work_ref[:, size:] = jnp.where(rows == columns, 1.0, 0.0).astype(jnp.float32)
    for first in range(0, size, BLOCK):
        last = first + BLOCK
        low = first // 128 * 128
        high = size + -(-last // 128) * 128
        small = factor_block(work_ref[first:last, first:last])
        solved = matmul(small, work_ref[first:last, low:high], ((1,), (0,)))
        work_ref[first:last, low:high] = solved
        if last < size:
            aligned = last // 128 * 128
            update = matmul(solved[:, aligned - low : size - low], solved, ((0,), (0,)))
            work_ref[last:, low:high] -= update[last - aligned :]


def factor_kernel(axes, cell_total, gram_ref, out_ref, parts, mine, work, send_sems, recv_sems):
    size = gram_ref.shape[0]
    if axes:
        (outer, outer_size), (inner, inner_size) = axes
        count = outer_size * inner_size
        share = size // count
        me = lax.axis_index(outer) * inner_size + lax.axis_index(inner)

        def peer(offset):
            index = lax.rem(me + offset, count)
            return index, {outer: index // inner_size, inner: lax.rem(index, inner_size)}

        barrier = pltpu.get_barrier_semaphore()
        for offset in range(1, count):
            pl.semaphore_signal(barrier, inc=1, device_id=peer(offset)[1], device_id_type=MESH)
        pl.semaphore_wait(barrier, count - 1)
        for offset in range(1, count):
            index, target = peer(offset)
            pltpu.make_async_remote_copy(
                src_ref=gram_ref.at[pl.ds(pl.multiple_of(index * share, share), share)],
                dst_ref=parts.at[offset - 1],
                send_sem=send_sems.at[0],
                recv_sem=recv_sems.at[0],
                device_id=target,
                device_id_type=MESH,
            ).start()
        own = pl.ds(pl.multiple_of(me * share, share), share)
        pltpu.make_async_copy(parts, parts, recv_sems.at[0]).wait()
        mine[...] = (jnp.sum(parts[...], axis=0) + gram_ref[own]) / cell_total
        for offset in range(1, count):
            index, target = peer(offset)
            pltpu.make_async_remote_copy(
                src_ref=mine,
                dst_ref=work.at[own, 0:size],
                send_sem=send_sems.at[1],
                recv_sem=recv_sems.at[1],
                device_id=target,
                device_id_type=MESH,
            ).start()
        pltpu.make_async_copy(parts, parts, send_sems.at[0]).wait()
        others = work.at[0 : size - share, 0:size]
        pltpu.make_async_copy(others, others, recv_sems.at[1]).wait()
        work[own, 0:size] = mine[...]
        pltpu.make_async_copy(parts, parts, send_sems.at[1]).wait()
    else:
        work[:, 0:size] = gram_ref[...] / cell_total
    inverse_factor(work, size)
    out_ref[...] = work[:, size:]


def inverse_of_gram(gram, cell_total):
    size = gram.shape[0]
    axes = tuple((name, lax.axis_size(name)) for name in ("band", "space"))
    count = axes[0][1] * axes[1][1]
    direct = size % (count * TILE) == 0
    if not direct:
        gram = lax.psum(gram, ("band", "space"))
    share = size // count if direct else TILE
    peers = count - 1 if direct else 1
    return pl.pallas_call(
        functools.partial(factor_kernel, axes if direct else (), float(cell_total)),
        out_shape=jax.ShapeDtypeStruct((size, size), jnp.float32),
        in_specs=[pl.BlockSpec(memory_space=pltpu.VMEM)],
        out_specs=pl.BlockSpec(memory_space=pltpu.VMEM),
        scratch_shapes=[
            pltpu.VMEM((peers, share, size), jnp.float32),
            pltpu.VMEM((share, size), jnp.float32),
            pltpu.VMEM((size, 2 * size), jnp.float32),
            pltpu.SemaphoreType.DMA((2,)),
            pltpu.SemaphoreType.DMA((2,)),
        ],
        compiler_params=pltpu.CompilerParams(
            collective_id=1 if direct else None, has_side_effects=direct
        ),
        name="gram_factor",
    )(gram)


FIRST = 4.0 / 3.0
SECOND = -1.0 / 12.0
REACH = 2


def filter_kernel(
    bands, spaces, states, base, shift_weights, out, grids, last, cells, base_send, base_recv,
    in_send, in_recv, keep_sems, halo_send, halo_recv, out_send, out_recv,
):
    planes, held, plane_cells = states.shape
    half = held // 2
    chunks = half // TILE
    span = 4 * planes
    share = plane_cells // bands
    band = lax.axis_index("band")
    space = lax.axis_index("space")
    side = lax.rem(space, 2)
    partner = space + 1 - 2 * side
    outward = space + 4 * side - 2
    across = space - 4 * side + 2
    ends = {0: space >= 2, 1: space < spaces - 2}
    towards = {0: space - 2, 1: space + 2}
    has_outward = jnp.logical_and(outward >= 0, outward < spaces)
    has_across = jnp.logical_and(across >= 0, across < spaces)

    def to(target_band, target_space):
        return {"band": target_band, "space": target_space}

    barrier = pltpu.get_barrier_semaphore()
    for turn in range(bands):
        target = lax.rem(band + turn, bands)
        if turn:
            pl.semaphore_signal(
                barrier, inc=1, device_id=to(target, space), device_id_type=MESH
            )
        pl.semaphore_signal(barrier, inc=1, device_id=to(target, partner), device_id_type=MESH)
    for end in (0, 1):

        @pl.when(ends[end])
        def _():
            pl.semaphore_signal(
                barrier, inc=1, device_id=to(band, towards[end]), device_id_type=MESH
            )

    below = jnp.minimum(space // 2, 1)
    above = jnp.minimum((spaces - 1 - space) // 2, 1)
    pl.semaphore_wait(barrier, 2 * bands - 1 + below + above)

    def slab(place):
        return pl.ds(place * planes, planes)

    def rows_of(part, chunk):
        return pl.ds(pl.multiple_of(part * half + chunk * TILE, TILE), TILE)

    def remote(source, landing, send_sem, recv_sem, target):
        return pltpu.make_async_remote_copy(
            src_ref=source,
            dst_ref=landing,
            send_sem=send_sem,
            recv_sem=recv_sem,
            device_id=to(band, target),
            device_id_type=MESH,
        )

    own, theirs = 1 + side, 2 - side
    own_landing, passed_landing = 3 * (1 - side), 3 * side
    base_sends = (
        remote(base, cells.at[own], base_send.at[0], base_recv.at[0], partner),
        remote(base, cells.at[own_landing], base_send.at[1], base_recv.at[1], outward),
        remote(cells.at[theirs], cells.at[passed_landing], base_send.at[2], base_recv.at[2], across),
    )
    base_keep = pltpu.make_async_copy(base, cells.at[own], base_send.at[3])
    enter, keep, halo_own, halo_passed = [], [], [], []
    for chunk in range(chunks):
        grid = grids.at[0, chunk]
        kept = states.at[:, rows_of(side, chunk)]
        enter.append(
            remote(
                states.at[:, rows_of(1 - side, chunk)], grid.at[slab(own)],
                in_send.at[chunk], in_recv.at[chunk], partner,
            )
        )
        keep.append(pltpu.make_async_copy(kept, grid.at[slab(own)], keep_sems.at[chunk]))
        halo_own.append(
            remote(
                kept, grid.at[slab(own_landing)],
                halo_send.at[0, chunk], halo_recv.at[0, chunk], outward,
            )
        )
        halo_passed.append(
            remote(
                grid.at[slab(theirs)], grid.at[slab(passed_landing)],
                halo_send.at[1, chunk], halo_recv.at[1, chunk], across,
            )
        )

    def begin(chunk):
        enter[chunk].start()

        @pl.when(has_outward)
        def _():
            if chunk == 0:
                base_sends[1].start()
            halo_own[chunk].start()

    base_sends[0].start()
    base_keep.start()
    for chunk in range(chunks):
        keep[chunk].start()
    for chunk in range(min(2, chunks)):
        begin(chunk)

    for place, missing in ((0, space < 2), (3, space >= spaces - 2)):

        @pl.when(missing)
        def _():
            cells[place] = jnp.zeros(cells.shape[1:], jnp.float32)
            for chunk in range(chunks):
                for plane in range(place * planes, (place + 1) * planes):
                    grids[0, chunk, plane] = jnp.zeros((TILE, plane_cells), jnp.float32)

    def apply(step, chunk):
        def plane(index, carry):
            here = index
            place = index // planes
            row = pl.ds(index - place * planes, 1)
            value = grids[step, chunk, here]
            near = grids[step, chunk, here - 1] + grids[step, chunk, here + 1]
            far = grids[step, chunk, here - 2] + grids[step, chunk, here + 2]
            total = cells[place, 0, row] * value
            total = total + cells[place, 1, row] * (FIRST * near + SECOND * far)
            for kind, stride in ((0, NZ), (1, 1)):
                part = None
                for position, offset in enumerate((-2, -1, 1, 2)):
                    amount = (-offset * stride) % plane_cells
                    moved = pltpu.roll(value, amount, axis=1)
                    number = kind * 4 + position
                    term = shift_weights[number : number + 1] * moved
                    part = term if part is None else part + term
                total = total + cells[place, 2 + kind, row] * part
            if step > 0:
                total = 2.0 * total - grids[step - 1, chunk, here]
            if step < DEGREE - 1:
                grids[step + 1, chunk, here] = total
            else:
                last[chunk, index - planes] = total
            return carry

        edge = REACH * (step + 1)
        lax.fori_loop(edge, span - edge, plane, 0)

    def leave(chunk):
        rows = pl.ds(pl.multiple_of(band * held + side * half + chunk * TILE, TILE), TILE)
        for turn in range(bands):
            target = lax.rem(band + turn, bands)
            columns = pl.ds(pl.multiple_of(target * share, share), share)
            for other in (1, 0):
                source = last.at[chunk, slab(side if other == 0 else 1 - side), :, columns]
                landing = out.at[:, rows, :]
                if turn == 0 and other == 0:
                    pltpu.make_async_copy(source, landing, out_recv.at[0]).start()
                else:
                    pltpu.make_async_remote_copy(
                        src_ref=source,
                        dst_ref=landing,
                        send_sem=out_send.at[0],
                        recv_sem=out_recv.at[0],
                        device_id=to(target, space if other == 0 else partner),
                        device_id_type=MESH,
                    ).start()

    def finish(chunk):
        @pl.when(has_across)
        def _():
            if chunk == 0:
                base_sends[1].wait_recv()
            halo_own[chunk].wait_recv()

        @pl.when(has_outward)
        def _():
            if chunk == 0:
                base_sends[2].wait_recv()
            halo_passed[chunk].wait_recv()

        for step in range(DEGREE):
            apply(step, chunk)
        leave(chunk)

    for chunk in range(chunks):
        if chunk == 0:
            base_keep.wait()
            base_sends[0].wait_recv()
        keep[chunk].wait()
        enter[chunk].wait_recv()

        @pl.when(has_across)
        def _():
            if chunk == 0:
                base_sends[2].start()
            halo_passed[chunk].start()

        if chunk + 2 < chunks:
            begin(chunk + 2)
        if chunk > 0:
            finish(chunk - 1)
    finish(chunks - 1)

    base_sends[0].wait_send()
    for chunk in range(chunks):
        enter[chunk].wait_send()

    @pl.when(has_outward)
    def _():
        base_sends[1].wait_send()
        for chunk in range(chunks):
            halo_own[chunk].wait_send()

    @pl.when(has_across)
    def _():
        base_sends[2].wait_send()
        for chunk in range(chunks):
            halo_passed[chunk].wait_send()

    pltpu.make_async_copy(out, out, out_recv.at[0]).wait()
    sent = out.at[:, 0 : out.shape[1] - out.shape[1] // (2 * bands), :]
    pltpu.make_async_copy(sent, sent, out_send.at[0]).wait()


def filtered_and_regrouped(states, base, shift_weights):
    planes, held, plane_cells = states.shape
    bands = lax.axis_size("band")
    spaces = lax.axis_size("space")
    chunks = held // 2 // TILE
    if planes != REACH * DEGREE:
        raise ValueError("slab depth")
    dma = pltpu.SemaphoreType.DMA
    return pl.pallas_call(
        functools.partial(filter_kernel, bands, spaces),
        out_shape=jax.ShapeDtypeStruct((planes, held * bands, plane_cells // bands), jnp.float32),
        in_specs=[
            pl.BlockSpec(memory_space=pl.ANY),
            pl.BlockSpec(memory_space=pltpu.VMEM),
            pl.BlockSpec(memory_space=pltpu.VMEM),
        ],
        out_specs=pl.BlockSpec(memory_space=pl.ANY),
        scratch_shapes=[
            pltpu.VMEM((DEGREE, chunks, 4 * planes, TILE, plane_cells), jnp.float32),
            pltpu.VMEM((chunks, 2 * planes, TILE, plane_cells), jnp.float32),
            pltpu.VMEM((4,) + base.shape, jnp.float32),
            dma((4,)),
            dma((3,)),
            dma((chunks,)),
            dma((chunks,)),
            dma((chunks,)),
            dma((2, chunks)),
            dma((2, chunks)),
            dma((1,)),
            dma((1,)),
        ],
        compiler_params=pltpu.CompilerParams(
            collective_id=0, has_side_effects=True, vmem_limit_bytes=40 * 2**20
        ),
        name="filter_regroup",
    )(states, base, shift_weights)


def coefficients(patch_ids, metric_table, potential):
    planes, plane_cells = potential.shape
    one_hot = (patch_ids[:, :, None] == jnp.arange(metric_table.shape[0], dtype=jnp.int32)).astype(
        jnp.float32
    )
    looked = jnp.einsum("xyp,pm->xym", one_hot, metric_table, precision=HIGHEST)
    metric = looked.reshape(planes, NY, 3, NZ).transpose(2, 0, 1, 3).reshape(3, planes, plane_cells)
    kinetic = metric * (-0.5 / HALF_WIDTH)
    centre = (potential - CENTRE) / HALF_WIDTH + WEIGHTS[2] * (
        kinetic[0] + kinetic[1] + kinetic[2]
    )
    base = jnp.concatenate([centre[None], kinetic], axis=0)
    return jnp.pad(base, ((0, 0), (0, -planes % TILE), (0, 0)))


def on_device(states, patch_ids, metric_table, potential):
    planes, plane_cells = potential.shape
    index = jnp.arange(plane_cells, dtype=jnp.int32)
    rows = []
    for place in (index // NZ, index % NZ):
        length = NY if not rows else NZ
        for offset, weight in ((-2, SECOND), (-1, FIRST), (1, FIRST), (2, SECOND)):
            inside = (place + offset >= 0) & (place + offset < length)
            rows.append(jnp.where(inside, weight, 0.0).astype(jnp.float32))
    shift_weights = jnp.stack(rows)
    base = coefficients(patch_ids, metric_table, potential)
    filtered = filtered_and_regrouped(states.transpose(1, 0, 2), base, shift_weights)
    cell_total = planes * plane_cells * lax.axis_size("space")
    local_gram = lax.dot_general(
        filtered[0], filtered[0], (((1,), (1,)), ((), ())), precision=HIGHEST,
        preferred_element_type=jnp.float32,
    )
    for plane in range(1, planes):
        local_gram = local_gram + lax.dot_general(
            filtered[plane], filtered[plane], (((1,), (1,)), ((), ())), precision=HIGHEST,
            preferred_element_type=jnp.float32,
        )
    inverse = inverse_of_gram(local_gram, cell_total)
    result = jnp.einsum(
        "ts,psc->ptc", inverse, filtered, precision=HIGHEST, preferred_element_type=jnp.float32
    )
    return result.transpose(1, 0, 2)


def solution(mesh):
    return jax.shard_map(
        on_device,
        mesh=mesh,
        in_specs=(P("band", "space", None), P("space", None), P(), P("space", None)),
        out_specs=P(None, "space", "band"),
        check_vma=False,
    )
```

```python
import functools

import jax
import jax.numpy as jnp
from jax import lax
from jax.experimental import pallas as pl
from jax.experimental.pallas import tpu as pltpu
from jax.sharding import PartitionSpec as P

DEGREE = 3
NY = 32
NZ = 32


CENTRE = 8.5
HALF_WIDTH = 7.5
OFFSETS = (-2, -1, 0, 1, 2)
WEIGHTS = (-1.0 / 12.0, 4.0 / 3.0, -2.5, 4.0 / 3.0, -1.0 / 12.0)


MESH = pl.DeviceIdType.MESH
HIGHEST = lax.Precision.HIGHEST
BLOCK = 64
TILE = 8


def matmul(left, right, dims):
    return lax.dot_general(
        left, right, (dims, ((), ())), precision=HIGHEST, preferred_element_type=jnp.float32
    )


def factor_block(diagonal):
    size = diagonal.shape[0]
    rows = lax.broadcasted_iota(jnp.int32, (size, size), 0)
    columns = lax.broadcasted_iota(jnp.int32, (size, size), 1)
    unit = jnp.where(rows == columns, 1.0, 0.0).astype(jnp.float32)
    work = jnp.concatenate([diagonal, unit], axis=1)
    width = work.shape[1]
    in_tile = lax.broadcasted_iota(jnp.int32, (TILE, width), 0)
    done = []
    for start in range(0, size, TILE):
        count = size - start
        row_in = lax.broadcasted_iota(jnp.int32, (count, width), 0)
        panel = [
            jnp.broadcast_to(work[:, start + k : start + k + 1], (count, width))
            for k in range(TILE)
        ]
        scale = jnp.zeros((TILE, width), jnp.float32)
        for k in range(TILE):
            pivot = panel[k][k : k + 1, :]
            inverse = 1.0 / pivot
            scale = jnp.where(in_tile == k, 1.0 / jnp.sqrt(pivot), scale)
            weight = jnp.where(row_in > k, panel[k] * inverse, 0.0)
            for later in range(k + 1, TILE):
                panel[later] = panel[later] - weight * panel[later][k : k + 1, :]
            work = work - weight * work[k : k + 1, :]
        done.append(work[:TILE] * scale)
        work = work[TILE:]
    return jnp.concatenate(done, axis=0)[:, size:]


def inverse_factor(work_ref, size):
    rows = lax.broadcasted_iota(jnp.int32, (size, size), 0)
    columns = lax.broadcasted_iota(jnp.int32, (size, size), 1)
    work_ref[:, size:] = jnp.where(rows == columns, 1.0, 0.0).astype(jnp.float32)
    for first in range(0, size, BLOCK):
        last = first + BLOCK
        low = first // 128 * 128
        high = size + -(-last // 128) * 128
        small = factor_block(work_ref[first:last, first:last])
        solved = matmul(small, work_ref[first:last, low:high], ((1,), (0,)))
        work_ref[first:last, low:high] = solved
        if last < size:
            aligned = last // 128 * 128
            update = matmul(solved[:, aligned - low : size - low], solved, ((0,), (0,)))
            work_ref[last:, low:high] -= update[last - aligned :]


def factor_kernel(
    bands, spaces, cell_total, gram_ref, out_ref, near, far, mine, final, work, send_sems, recv_sems
):
    size = gram_ref.shape[0]
    if bands:
        near_count, far_count = 2 * bands, spaces // 2
        share = size // near_count
        band, space = lax.axis_index("band"), lax.axis_index("space")
        line = space // 2
        side = space - 2 * line
        place = 2 * band + side
        own = pl.ds(pl.multiple_of(place * share, share), share)

        def near_peer(offset):
            index = lax.rem(place + offset, near_count)
            return index, {"band": index // 2, "space": 2 * line + lax.rem(index, 2)}

        def far_peer(offset):
            return {"band": band, "space": 2 * lax.rem(line + offset, far_count) + side}

        def send(source, landing, stage, target):
            pltpu.make_async_remote_copy(
                src_ref=source,
                dst_ref=landing,
                send_sem=send_sems.at[stage],
                recv_sem=recv_sems.at[stage],
                device_id=target,
                device_id_type=MESH,
            ).start()

        barrier = pltpu.get_barrier_semaphore()
        for offset in range(1, near_count):
            pl.semaphore_signal(
                barrier, inc=1, device_id=near_peer(offset)[1], device_id_type=MESH
            )
        for offset in range(1, far_count):
            pl.semaphore_signal(barrier, inc=1, device_id=far_peer(offset), device_id_type=MESH)
        pl.semaphore_wait(barrier, near_count + far_count - 2)
        for offset in range(1, near_count):
            index, target = near_peer(offset)
            rows = pl.ds(pl.multiple_of(index * share, share), share)
            send(gram_ref.at[rows], near.at[offset - 1], 0, target)
        pltpu.make_async_copy(near, near, recv_sems.at[0]).wait()
        mine[...] = jnp.sum(near[...], axis=0) + gram_ref[own]
        for offset in range(1, far_count):
            send(mine, far.at[line], 1, far_peer(offset))
        others = far.at[0 : far_count - 1]
        pltpu.make_async_copy(others, others, recv_sems.at[1]).wait()
        far[line] = mine[...]
        final[...] = jnp.sum(far[...], axis=0) / cell_total
        for offset in range(1, near_count):
            send(final, work.at[own, 0:size], 2, near_peer(offset)[1])
        rest = work.at[0 : size - share, 0:size]
        pltpu.make_async_copy(rest, rest, recv_sems.at[2]).wait()
        work[own, 0:size] = final[...]
        pltpu.make_async_copy(near, near, send_sems.at[0]).wait()
        pltpu.make_async_copy(others, others, send_sems.at[1]).wait()
        pltpu.make_async_copy(near, near, send_sems.at[2]).wait()
    else:
        work[:, 0:size] = gram_ref[...] / cell_total
    inverse_factor(work, size)
    out_ref[...] = work[:, size:]


def inverse_of_gram(gram, cell_total):
    size = gram.shape[0]
    bands, spaces = lax.axis_size("band"), lax.axis_size("space")
    direct = size % (2 * bands * TILE) == 0 and spaces % 2 == 0 and spaces >= 4
    if not direct:
        gram = lax.psum(gram, ("band", "space"))
        bands, spaces = 0, 4
    near_count = 2 * max(bands, 1)
    share = size // near_count
    return pl.pallas_call(
        functools.partial(factor_kernel, bands, spaces, float(cell_total)),
        out_shape=jax.ShapeDtypeStruct((size, size), jnp.float32),
        in_specs=[pl.BlockSpec(memory_space=pltpu.VMEM)],
        out_specs=pl.BlockSpec(memory_space=pltpu.VMEM),
        scratch_shapes=[
            pltpu.VMEM((near_count - 1, share, size), jnp.float32),
            pltpu.VMEM((spaces // 2, share, size), jnp.float32),
            pltpu.VMEM((share, size), jnp.float32),
            pltpu.VMEM((share, size), jnp.float32),
            pltpu.VMEM((size, 2 * size), jnp.float32),
            pltpu.SemaphoreType.DMA((3,)),
            pltpu.SemaphoreType.DMA((3,)),
        ],
        compiler_params=pltpu.CompilerParams(
            collective_id=1 if direct else None, has_side_effects=direct
        ),
        name="gram_factor",
    )(gram)


FIRST = 4.0 / 3.0
SECOND = -1.0 / 12.0
REACH = 2


def filter_kernel(
    bands, spaces, states, base, shift_weights, out, grids, last, cells, base_send, base_recv,
    in_send, in_recv, keep_sems, halo_send, halo_recv, out_send, out_recv,
):
    planes, held, plane_cells = states.shape
    half = held // 2
    chunks = half // TILE
    span = 4 * planes
    share = plane_cells // bands
    band = lax.axis_index("band")
    space = lax.axis_index("space")
    side = lax.rem(space, 2)
    partner = space + 1 - 2 * side
    outward = space + 4 * side - 2
    across = space - 4 * side + 2
    ends = {0: space >= 2, 1: space < spaces - 2}
    towards = {0: space - 2, 1: space + 2}
    has_outward = jnp.logical_and(outward >= 0, outward < spaces)
    has_across = jnp.logical_and(across >= 0, across < spaces)

    def to(target_band, target_space):
        return {"band": target_band, "space": target_space}

    barrier = pltpu.get_barrier_semaphore()
    for turn in range(bands):
        target = lax.rem(band + turn, bands)
        if turn:
            pl.semaphore_signal(
                barrier, inc=1, device_id=to(target, space), device_id_type=MESH
            )
        pl.semaphore_signal(barrier, inc=1, device_id=to(target, partner), device_id_type=MESH)
    for end in (0, 1):

        @pl.when(ends[end])
        def _():
            pl.semaphore_signal(
                barrier, inc=1, device_id=to(band, towards[end]), device_id_type=MESH
            )

    below = jnp.minimum(space // 2, 1)
    above = jnp.minimum((spaces - 1 - space) // 2, 1)
    pl.semaphore_wait(barrier, 2 * bands - 1 + below + above)

    def slab(place):
        return pl.ds(place * planes, planes)

    def rows_of(part, chunk):
        return pl.ds(pl.multiple_of(part * half + chunk * TILE, TILE), TILE)

    def remote(source, landing, send_sem, recv_sem, target):
        return pltpu.make_async_remote_copy(
            src_ref=source,
            dst_ref=landing,
            send_sem=send_sem,
            recv_sem=recv_sem,
            device_id=to(band, target),
            device_id_type=MESH,
        )

    own, theirs = 1 + side, 2 - side
    own_landing, passed_landing = 3 * (1 - side), 3 * side
    base_sends = (
        remote(base, cells.at[own], base_send.at[0], base_recv.at[0], partner),
        remote(base, cells.at[own_landing], base_send.at[1], base_recv.at[1], outward),
        remote(cells.at[theirs], cells.at[passed_landing], base_send.at[2], base_recv.at[2], across),
    )
    base_keep = pltpu.make_async_copy(base, cells.at[own], base_send.at[3])
    enter, keep, halo_own, halo_passed = [], [], [], []
    for chunk in range(chunks):
        grid = grids.at[0, chunk]
        kept = states.at[:, rows_of(side, chunk)]
        enter.append(
            remote(
                states.at[:, rows_of(1 - side, chunk)], grid.at[slab(own)],
                in_send.at[chunk], in_recv.at[chunk], partner,
            )
        )
        keep.append(pltpu.make_async_copy(kept, grid.at[slab(own)], keep_sems.at[chunk]))
        halo_own.append(
            remote(
                kept, grid.at[slab(own_landing)],
                halo_send.at[0, chunk], halo_recv.at[0, chunk], outward,
            )
        )
        halo_passed.append(
            remote(
                grid.at[slab(theirs)], grid.at[slab(passed_landing)],
                halo_send.at[1, chunk], halo_recv.at[1, chunk], across,
            )
        )

    def begin(chunk):
        enter[chunk].start()

        @pl.when(has_outward)
        def _():
            if chunk == 0:
                base_sends[1].start()
            halo_own[chunk].start()

    base_sends[0].start()
    base_keep.start()
    for chunk in range(chunks):
        keep[chunk].start()
    for chunk in range(min(2, chunks)):
        begin(chunk)

    for place, missing in ((0, space < 2), (3, space >= spaces - 2)):

        @pl.when(missing)
        def _():
            cells[place] = jnp.zeros(cells.shape[1:], jnp.float32)
            for chunk in range(chunks):
                for plane in range(place * planes, (place + 1) * planes):
                    grids[0, chunk, plane] = jnp.zeros((TILE, plane_cells), jnp.float32)

    def apply(step, chunk):
        edge = REACH * (step + 1)

        def stencil(here, around):
            place = here // planes
            row = pl.ds(here - place * planes, 1)
            value = around[2]
            near = around[1] + around[3]
            far = around[0] + around[4]
            total = cells[place, 0, row] * value
            total = total + cells[place, 1, row] * (FIRST * near + SECOND * far)
            for kind, stride in ((0, NZ), (1, 1)):
                part = None
                for position, offset in enumerate((-2, -1, 1, 2)):
                    amount = (-offset * stride) % plane_cells
                    moved = pltpu.roll(value, amount, axis=1)
                    number = kind * 4 + position
                    term = shift_weights[number : number + 1] * moved
                    part = term if part is None else part + term
                total = total + cells[place, 2 + kind, row] * part
            if step > 0:
                total = 2.0 * total - grids[step - 1, chunk, here]
            return total

        def two_planes(pair, carry):
            first = edge + 2 * pair
            around = [grids[step, chunk, first + shift] for shift in range(-2, 4)]
            totals = [stencil(first, around[:5]), stencil(first + 1, around[1:])]
            for shift, total in enumerate(totals):
                if step < DEGREE - 1:
                    grids[step + 1, chunk, first + shift] = total
                else:
                    last[chunk, first + shift - planes] = total
            return carry

        lax.fori_loop(0, span // 2 - edge, two_planes, 0)

    def leave(chunk):
        rows = pl.ds(pl.multiple_of(band * held + side * half + chunk * TILE, TILE), TILE)
        for turn in range(bands):
            target = lax.rem(band + turn, bands)
            columns = pl.ds(pl.multiple_of(target * share, share), share)
            for other in (1, 0):
                source = last.at[chunk, slab(side if other == 0 else 1 - side), :, columns]
                landing = out.at[:, rows, :]
                if turn == 0 and other == 0:
                    pltpu.make_async_copy(source, landing, out_recv.at[0]).start()
                else:
                    pltpu.make_async_remote_copy(
                        src_ref=source,
                        dst_ref=landing,
                        send_sem=out_send.at[0],
                        recv_sem=out_recv.at[0],
                        device_id=to(target, space if other == 0 else partner),
                        device_id_type=MESH,
                    ).start()

    def finish(chunk):
        @pl.when(has_across)
        def _():
            if chunk == 0:
                base_sends[1].wait_recv()
            halo_own[chunk].wait_recv()

        @pl.when(has_outward)
        def _():
            if chunk == 0:
                base_sends[2].wait_recv()
            halo_passed[chunk].wait_recv()

        for step in range(DEGREE):
            apply(step, chunk)
        leave(chunk)

    for chunk in range(chunks):
        if chunk == 0:
            base_keep.wait()
            base_sends[0].wait_recv()
        keep[chunk].wait()
        enter[chunk].wait_recv()

        @pl.when(has_across)
        def _():
            if chunk == 0:
                base_sends[2].start()
            halo_passed[chunk].start()

        if chunk + 2 < chunks:
            begin(chunk + 2)
        if chunk > 0:
            finish(chunk - 1)
    finish(chunks - 1)

    base_sends[0].wait_send()
    for chunk in range(chunks):
        enter[chunk].wait_send()

    @pl.when(has_outward)
    def _():
        base_sends[1].wait_send()
        for chunk in range(chunks):
            halo_own[chunk].wait_send()

    @pl.when(has_across)
    def _():
        base_sends[2].wait_send()
        for chunk in range(chunks):
            halo_passed[chunk].wait_send()

    pltpu.make_async_copy(out, out, out_recv.at[0]).wait()
    sent = out.at[:, 0 : out.shape[1] - out.shape[1] // (2 * bands), :]
    pltpu.make_async_copy(sent, sent, out_send.at[0]).wait()


def filtered_and_regrouped(states, base, shift_weights):
    planes, held, plane_cells = states.shape
    bands = lax.axis_size("band")
    spaces = lax.axis_size("space")
    chunks = held // 2 // TILE
    if planes != REACH * DEGREE:
        raise ValueError("slab depth")
    dma = pltpu.SemaphoreType.DMA
    return pl.pallas_call(
        functools.partial(filter_kernel, bands, spaces),
        out_shape=jax.ShapeDtypeStruct((planes, held * bands, plane_cells // bands), jnp.float32),
        in_specs=[
            pl.BlockSpec(memory_space=pl.ANY),
            pl.BlockSpec(memory_space=pltpu.VMEM),
            pl.BlockSpec(memory_space=pltpu.VMEM),
        ],
        out_specs=pl.BlockSpec(memory_space=pl.ANY),
        scratch_shapes=[
            pltpu.VMEM((DEGREE, chunks, 4 * planes, TILE, plane_cells), jnp.float32),
            pltpu.VMEM((chunks, 2 * planes, TILE, plane_cells), jnp.float32),
            pltpu.VMEM((4,) + base.shape, jnp.float32),
            dma((4,)),
            dma((3,)),
            dma((chunks,)),
            dma((chunks,)),
            dma((chunks,)),
            dma((2, chunks)),
            dma((2, chunks)),
            dma((1,)),
            dma((1,)),
        ],
        compiler_params=pltpu.CompilerParams(
            collective_id=0, has_side_effects=True, vmem_limit_bytes=40 * 2**20
        ),
        name="filter_regroup",
    )(states, base, shift_weights)


def coefficients(patch_ids, metric_table, potential):
    planes, plane_cells = potential.shape
    one_hot = (patch_ids[:, :, None] == jnp.arange(metric_table.shape[0], dtype=jnp.int32)).astype(
        jnp.float32
    )
    looked = jnp.einsum("xyp,pm->xym", one_hot, metric_table, precision=HIGHEST)
    metric = looked.reshape(planes, NY, 3, NZ).transpose(2, 0, 1, 3).reshape(3, planes, plane_cells)
    kinetic = metric * (-0.5 / HALF_WIDTH)
    centre = (potential - CENTRE) / HALF_WIDTH + WEIGHTS[2] * (
        kinetic[0] + kinetic[1] + kinetic[2]
    )
    base = jnp.concatenate([centre[None], kinetic], axis=0)
    return jnp.pad(base, ((0, 0), (0, -planes % TILE), (0, 0)))


def on_device(states, patch_ids, metric_table, potential):
    planes, plane_cells = potential.shape
    index = jnp.arange(plane_cells, dtype=jnp.int32)
    rows = []
    for place in (index // NZ, index % NZ):
        length = NY if not rows else NZ
        for offset, weight in ((-2, SECOND), (-1, FIRST), (1, FIRST), (2, SECOND)):
            inside = (place + offset >= 0) & (place + offset < length)
            rows.append(jnp.where(inside, weight, 0.0).astype(jnp.float32))
    shift_weights = jnp.stack(rows)
    base = coefficients(patch_ids, metric_table, potential)
    filtered = filtered_and_regrouped(states.transpose(1, 0, 2), base, shift_weights)
    cell_total = planes * plane_cells * lax.axis_size("space")
    local_gram = lax.dot_general(
        filtered[0], filtered[0], (((1,), (1,)), ((), ())), precision=HIGHEST,
        preferred_element_type=jnp.float32,
    )
    for plane in range(1, planes):
        local_gram = local_gram + lax.dot_general(
            filtered[plane], filtered[plane], (((1,), (1,)), ((), ())), precision=HIGHEST,
            preferred_element_type=jnp.float32,
        )
    inverse = inverse_of_gram(local_gram, cell_total)
    result = jnp.einsum(
        "ts,psc->ptc", inverse, filtered, precision=HIGHEST, preferred_element_type=jnp.float32
    )
    return result.transpose(1, 0, 2)


def solution(mesh):
    return jax.shard_map(
        on_device,
        mesh=mesh,
        in_specs=(P("band", "space", None), P("space", None), P(), P("space", None)),
        out_specs=P(None, "space", "band"),
        check_vma=False,
    )
```
